32 devices in a mesh: tile: 4 (over x, core), tm: 8 (over z, y).
Axes of the slice: x: 2, y: 2, z: 4, core: 2. Of those that a mesh axis runs over, the one named last changes fastest.
Arguments:
- movie: bfloat16 [128, 256, 512], P('tile', None, 'tm'), may hold values from -6 to 6
- footprints: bfloat16 [32, 4, 32, 32, 128], P('tile'), may hold values from -0.5 to 0.5
- support: int32 [32, 4], P('tile'), may hold values from -1 to 31, as said below
- cycle_offsets: int32 [48, 2], replicated, may hold values from -8 to 8, as said below
- cycle_weights: float32 [48, 128, 256], P(None, 'tile'), may hold values from -0.875 to 0.875
- owner_map: int32 [32], replicated, may hold values from 0 to 31, each once
- traces_old: bfloat16 [4096, 512], P(('tile', 'tm')), may hold values from 0 to 2
- taps: float32 [129], replicated, may hold values from -0.5 to 0.5
Outputs:
- residual: bfloat16 [128, 256, 512], P('tile', None, 'tm')
- traces_new: bfloat16 [4096, 512], P(('tile', 'tm'))
The draws below stay inside these ranges and needn't reach their ends.
Inputs may be any that keep to these rules, and one draw needn't show every extreme that they name: `support`: in every row the live slots come first and name distinct blocks; -1 marks the empty slots. Every tile has 1 to 4 live slots, and every tile row (the 8 tiles t with equal t // 8) has exactly 20 live slots in all. `cycle_offsets`: rows are distinct (row offset, column offset) pairs; each has max(|row offset|, |column offset|) between 6 and 8; one row offset is 8 and one is -8. `owner_map`: each block has its own position.
All inputs are finite; a program needn't handle non-finite values.
Results may differ from the reference program's by a relative error of at most 0.0075.
Values may be sent and summed in bfloat16 or wider, within the bound.
No kernel may reach another device: no remote copies, remote signals or barrier semaphores. Data moves between devices by JAX's collectives and lax.ppermute only.
A program may use at most 128 MiB of HBM per device.

```python
import jax
import jax.numpy as jnp
from jax import lax

TILE = 32
TILES_DEV = 8
F_DEV = 64
BLOCK = 128
NBLK = 32
KSLOTS = 4
RAD = 8
CYCLE = 48
HALF = 64
ROWS = 128
COLS = 256
FRAMES = 512
NEURONS = 4096
TILES = 32
NTAP = 129
LIVE_DEV = 20
N_TILE = 4
N_TM = 8


def draw_footprints(key, part):
    base_key, neuron_key, pixel_key = jax.random.split(jax.random.fold_in(key, 37), 3)
    draw_shape = (TILES, KSLOTS, TILE, TILE, BLOCK)
    base_values = jnp.clip(jax.random.normal(base_key, draw_shape, jnp.float32), -4.0, 4.0)
    neuron_scale = jnp.exp(jax.random.uniform(neuron_key, (TILES, KSLOTS, 1, 1, BLOCK), jnp.float32, jnp.log(0.3), jnp.log(3.0)))
    pixel_scale = jnp.exp(jax.random.uniform(pixel_key, (TILES, 1, TILE, TILE, 1), jnp.float32, jnp.log(0.5), jnp.log(2.0)))
    return jnp.clip(base_values * neuron_scale * pixel_scale / 32.0, -0.5, 0.5).astype(jnp.bfloat16)


def draw_support(key, part):
    count_key, block_key = jax.random.split(jax.random.fold_in(key, 11))
    groups_total = TILES // TILES_DEV
    extra_total = TILES_DEV * (KSLOTS - 1)
    count_keys = jax.random.split(count_key, groups_total)
    chosen_order = jax.vmap(lambda one_key: jax.random.permutation(one_key, extra_total))(count_keys)
    chosen = (chosen_order < LIVE_DEV - TILES_DEV).astype(jnp.int32)
    counts = 1 + jnp.sum(chosen.reshape(groups_total, TILES_DEV, KSLOTS - 1), axis=2).reshape(TILES)
    block_keys = jax.random.split(block_key, TILES)
    orders = jax.vmap(lambda one_key: jax.random.permutation(one_key, NBLK))(block_keys)[:, :KSLOTS]
    slot_number = jnp.arange(KSLOTS, dtype=jnp.int32)[None, :]
    return jnp.where(slot_number < counts[:, None], orders, -1).astype(jnp.int32)


def draw_cycle_offsets(key, part):
    score_key, top_key, bottom_key = jax.random.split(jax.random.fold_in(key, 23), 3)
    span_cells = 2 * RAD + 1
    cell_ids = jnp.arange(span_cells * span_cells, dtype=jnp.int32)
    delta_row = cell_ids // span_cells - RAD
    delta_col = cell_ids % span_cells - RAD
    radius = jnp.maximum(jnp.abs(delta_row), jnp.abs(delta_col))
    usable = (radius >= RAD - 2) & (jnp.abs(delta_row) < RAD)
    scores = jax.random.randint(score_key, (span_cells * span_cells,), 0, 1 << 20) * (span_cells * span_cells) + cell_ids
    scores = jnp.where(usable, scores, 1 << 30)
    picked = jnp.argsort(scores)[:CYCLE - 2]
    top_col = jax.random.randint(top_key, (1,), -RAD, RAD + 1)
    bottom_col = jax.random.randint(bottom_key, (1,), -RAD, RAD + 1)
    rows_part = jnp.concatenate([delta_row[picked], jnp.array([RAD, -RAD], jnp.int32)])
    cols_part = jnp.concatenate([delta_col[picked], top_col, bottom_col])
    return jnp.stack([rows_part, cols_part], axis=1).astype(jnp.int32)


def block_scale(rng, extent, cuts, low, high):
    factor_of = 1.0
    for axis_at, shards_of in cuts:
        heights = jax.random.uniform(jax.random.fold_in(jax.random.fold_in(rng, 6), axis_at), (shards_of,), jnp.float32, low / len(cuts), high / len(cuts))
        factor_of = factor_of * jnp.repeat(jnp.exp(heights), extent[axis_at] // shards_of).reshape((-1,) + (1,) * (len(extent) - 1 - axis_at))
    return factor_of


def gaussian(key, shape, deviation, bound, shards=(), kind=jnp.bfloat16):
    entries = jax.random.normal(key, shape, jnp.float32) * deviation
    if len(shards) > 0:
        entries = block_scale(key, shape, shards, -0.22, 0.18) * entries
    return jnp.clip(entries, min=-bound, max=bound).astype(kind)


def setup_inputs(seed: int = 0) -> dict:
    splits = jax.random.split(jax.random.key(seed), 9)
    movie = gaussian(splits[0], (ROWS, COLS, FRAMES), 1.0, 6.0, ((0, 4), (2, 8)))
    footprints = draw_footprints(jax.random.fold_in(splits[8], 71), 0)
    support = draw_support(jax.random.fold_in(splits[8], 71), 0)
    cycle_offsets = draw_cycle_offsets(jax.random.fold_in(splits[8], 71), 0)
    cycle_weights = gaussian(splits[4], (CYCLE, ROWS, COLS), CYCLE ** -0.5, 0.875, ((1, 4),), jnp.float32)
    owner_map = jax.random.permutation(splits[5], NBLK).astype(jnp.int32)
    traces_old = jnp.clip(2.0 * jax.random.uniform(splits[6], (NEURONS, FRAMES), jnp.float32) ** block_scale(splits[6], (NEURONS, FRAMES), ((0, 32),), -0.2, 0.2), 0.0, 2.0).astype(jnp.bfloat16)
    taps = gaussian(splits[7], (NTAP,), NTAP ** -0.5, 0.5, (), jnp.float32)
    return {"movie": movie, "footprints": footprints, "support": support, "cycle_offsets": cycle_offsets, "cycle_weights": cycle_weights, "owner_map": owner_map, "traces_old": traces_old, "taps": taps}


ridge_term = 1.0
highest = lax.Precision.HIGHEST


def cycle_pass(field_in, cycle_weights, cycle_offsets):
    row_count, col_count, frames = field_in.shape
    padded = jnp.pad(field_in.astype(jnp.float32), ((RAD, RAD), (RAD, RAD), (0, 0)))
    running = jnp.zeros((row_count, col_count, frames), jnp.float32)
    for cycle_index in range(CYCLE):
        start_row = (RAD + cycle_offsets[cycle_index, 0]).astype(jnp.int32)
        start_col = (RAD + cycle_offsets[cycle_index, 1]).astype(jnp.int32)
        shifted = lax.dynamic_slice(padded, (start_row, start_col, jnp.zeros((), jnp.int32)), (row_count, col_count, frames))
        running = running + cycle_weights[cycle_index][:, :, None] * shifted
    return running


def neural_part(footprint_f, live_slot, position, trace_block):
    frame_count = trace_block.shape[1]
    blocks = trace_block.reshape(NBLK, BLOCK, frame_count)
    picked = blocks[position.reshape(-1)].reshape(N_TILE, TILES_DEV, KSLOTS, BLOCK, frame_count)
    picked = jnp.where(live_slot.reshape(N_TILE, TILES_DEV, KSLOTS)[:, :, :, None, None], picked.astype(jnp.float32), 0.0)
    neural_image = jnp.einsum('gtkrcn,gtknf->grtcf', footprint_f, picked, precision=highest)
    return neural_image.reshape(ROWS, COLS, frame_count)


def reference(movie, footprints, support, cycle_offsets, cycle_weights, owner_map, traces_old, taps):
    live_slot = support >= 0
    position = owner_map[jnp.maximum(support, 0)].astype(jnp.int32)
    footprint_f = footprints.astype(jnp.float32).reshape(N_TILE, TILES_DEV, KSLOTS, TILE, TILE, BLOCK)
    block_ids = jnp.arange(NBLK, dtype=jnp.int32)
    selector = ((position.reshape(-1)[None, :] == block_ids[:, None]) & live_slot.reshape(-1)[None, :]).astype(jnp.float32)
    movie_blocks = movie.reshape(ROWS, COLS, N_TM, F_DEV).transpose(2, 0, 1, 3)
    old_blocks = traces_old.reshape(NEURONS, N_TM, F_DEV).transpose(1, 0, 2)

    def first_pass(carried):
        frame_movie, frame_traces = carried
        neural_old = neural_part(footprint_f, live_slot, position, frame_traces)
        first_res = (frame_movie.astype(jnp.float32) - neural_old).astype(jnp.bfloat16)
        second_res = (first_res.astype(jnp.float32) - cycle_pass(first_res, cycle_weights, cycle_offsets)).astype(jnp.bfloat16)
        third_res = (second_res.astype(jnp.float32) - cycle_pass(second_res, cycle_weights, cycle_offsets)).astype(jnp.bfloat16)
        tile_view = third_res.astype(jnp.float32).reshape(N_TILE, TILE, TILES_DEV, TILE, F_DEV)
        slot_proj = jnp.einsum('gtkrcn,grtcf->gtknf', footprint_f, tile_view, precision=highest)
        owned_sums = jnp.dot(selector, slot_proj.reshape(TILES * KSLOTS, BLOCK * F_DEV), precision=highest)
        return third_res, owned_sums.reshape(NEURONS, F_DEV)

    cleaned, projected = lax.map(first_pass, (movie_blocks, old_blocks))
    projected = projected.transpose(1, 0, 2).reshape(NEURONS, FRAMES)
    squares = jnp.sum(footprint_f * footprint_f, axis=(3, 4)).reshape(TILES * KSLOTS, BLOCK)
    norm_sums = jnp.dot(selector, squares, precision=highest).reshape(NEURONS)
    update = traces_old.astype(jnp.float32) + projected / (norm_sums[:, None] + ridge_term)
    padded = jnp.pad(update, ((0, 0), (HALF, HALF)))
    filtered = jnp.zeros((NEURONS, FRAMES), jnp.float32)
    for tap_index in range(2 * HALF + 1):
        begin_col = 2 * HALF - tap_index
        filtered = filtered + taps[tap_index] * padded[:, begin_col:begin_col + FRAMES]
    traces_new = jnp.maximum(filtered, 0.0).astype(jnp.bfloat16)
    new_blocks = traces_new.reshape(NEURONS, N_TM, F_DEV).transpose(1, 0, 2)

    def second_pass(carried):
        cleaned_block, frame_old, frame_new = carried
        image_old = neural_part(footprint_f, live_slot, position, frame_old)
        image_new = neural_part(footprint_f, live_slot, position, frame_new)
        return (cleaned_block.astype(jnp.float32) + image_old - image_new).astype(jnp.bfloat16)

    residual = lax.map(second_pass, (cleaned, old_blocks, new_blocks))
    residual = residual.transpose(1, 2, 0, 3).reshape(ROWS, COLS, FRAMES)
    return residual, traces_new
```

```python
import functools

import jax
import jax.numpy as jnp
from jax import lax
from jax.experimental import pallas as pl
from jax.experimental.pallas import tpu as pltpu
from jax.sharding import PartitionSpec as P

RAD = 8
LANES = 128
ROW_STEP = 8
AHEAD = 4
FIRST_VMEM = 53
FINAL_VMEM = 53
TAP_GROUP = 4
MIB = 1024 * 1024
FRAME_PARTS = 2
ridge_term = 1.0
highest = lax.Precision.HIGHEST
bf16 = jnp.bfloat16
f32 = jnp.float32
NT = (((1,), (1,)), ((), ()))
NN = (((1,), (0,)), ((), ()))

smem = pl.BlockSpec(memory_space=pltpu.SMEM)
vmem = pl.BlockSpec(memory_space=pltpu.VMEM)
anywhere = pl.BlockSpec(memory_space=pl.ANY)


def swap_groups(parts, width):
    count = len(parts)
    lane = lax.broadcasted_iota(jnp.int32, parts[0].shape, 1)
    dist = count // 2
    while dist >= 1:
        upper = (lane // (width * dist)) % 2 == 1
        out = list(parts)
        for a in range(count):
            if a & dist:
                continue
            low, high = parts[a], parts[a | dist]
            out[a] = jnp.where(upper, pltpu.roll(high, width * dist, 1), low)
            out[a | dist] = jnp.where(upper, high, pltpu.roll(low, LANES - width * dist, 1))
        parts = out
        dist //= 2
    return parts


def slot_position(support_ref, owner_ref, slot):
    slots = support_ref.shape[0]
    block = support_ref[slot % slots, slot // slots]
    return jnp.where(block >= 0, owner_ref[jnp.maximum(block, 0)], -1)


def place_of(position, here, tile_count, share):
    apart = (position // share) ^ here
    bits = tile_count.bit_length() - 1
    rank = sum(((apart >> b) & 1) << (bits - 1 - b) for b in range(bits))
    return rank * share + position % share


def gather_lhs(support_ref, owner_ref, here_ref, pieces, lhs_ref):
    tile_count = len(pieces[0])
    share = pieces[0][0].shape[0]
    for slot in range(2 * lhs_ref.shape[0]):
        position = slot_position(support_ref, owner_ref, slot)
        live = position >= 0
        index = jnp.maximum(position, 0)
        apart = (index // share) ^ here_ref[0]
        row = index % share
        parts = []
        for refs in pieces:
            value = refs[0][row]
            for rank in range(1, tile_count):
                value = jnp.where(apart == rank, refs[rank][row], value)
            parts.append(jnp.where(live, value, jnp.zeros_like(value)))
        value = parts[0] if len(parts) == 1 else jnp.concatenate(parts, axis=0)
        block = value.shape[1]
        lhs_ref[slot // 2, :, (slot % 2) * block : (slot % 2 + 1) * block] = value


def neural_rows(lhs_ref, chunk_ref):
    tiles, slots = chunk_ref.shape[:2]
    images = []
    for t in range(tiles):
        image = None
        for k in range(0, slots, 2):
            rhs = jnp.concatenate([chunk_ref[t, k + i] for i in range(2)], axis=1)
            part = lax.dot_general(
                lhs_ref[(t * slots + k) // 2], rhs, NT, preferred_element_type=f32
            )
            image = part if image is None else image + part
        images.append(image)
    return images


class Copies:
    def __init__(self, parts):
        self.parts = parts

    def start(self):
        for part in self.parts:
            part.start()

    def wait(self):
        for part in self.parts:
            part.wait()


def chunk_copies(tile, prints_ref, chunks_ref, sems):
    size = ROW_STEP * tile
    return [
        Copies(
            [
                pltpu.make_async_copy(
                    prints_ref.at[t, :, pl.ds(c * size, size), :], chunks_ref.at[c, t], sems.at[c, t]
                )
                for t in range(chunks_ref.shape[1])
            ]
        )
        for c in range(chunks_ref.shape[0])
    ]


def field_copies(field_ref, chunks_ref, sems):
    return [
        pltpu.make_async_copy(
            field_ref.at[pl.ds(c * ROW_STEP, ROW_STEP)], chunks_ref.at[c], sems.at[c]
        )
        for c in range(chunks_ref.shape[0])
    ]


def image_rows(tile, images, finish):
    group = LANES // tile
    for h in range(ROW_STEP // group):
        sides = []
        for g in range(0, len(images), group):
            cut = [im[:, h * LANES : (h + 1) * LANES] for im in images[g : g + group]]
            sides.append(swap_groups(cut, tile))
        for r in range(group):
            finish(h * group + r, jnp.concatenate([side[r] for side in sides], axis=1))


def write_edges(odd, first_rows, last_rows, inner_ref, outer_ref):
    @pl.when(odd == 1)
    def _():
        inner_ref[...] = last_rows()
        outer_ref[...] = first_rows()

    @pl.when(odd != 1)
    def _():
        inner_ref[...] = first_rows()
        outer_ref[...] = last_rows()


def first_kernel(tile, tile_count, support_ref, owner_ref, here_ref, split_ref, movie_ref, prints_ref, *refs):
    pieces = refs[:tile_count]
    out_ref, inner_ref, outer_ref, prints_buf, movie_buf, lhs_ref, prints_sem, movie_sem = refs[tile_count:]
    copies = chunk_copies(tile, prints_ref, prints_buf, prints_sem)
    movies = field_copies(movie_ref, movie_buf, movie_sem)
    for c in range(AHEAD):
        movies[c].start()
        copies[c].start()
    gather_lhs(support_ref, owner_ref, here_ref, (pieces,), lhs_ref)
    for c in range(len(copies)):
        movies[c].wait()
        copies[c].wait()
        if c + AHEAD < len(copies):
            movies[c + AHEAD].start()
            copies[c + AHEAD].start()
        images = neural_rows(lhs_ref, prints_buf.at[c])

        def finish(row, image):
            value = (movie_buf[c, row].astype(f32) - image).astype(bf16)
            moved = lax.dot_general(value, split_ref[...], NN, preferred_element_type=f32)
            out_ref[c * ROW_STEP + row] = moved.astype(bf16)

        image_rows(tile, images, finish)
    rows = out_ref.shape[0]
    write_edges(
        here_ref[0] % 2,
        lambda: out_ref[:RAD],
        lambda: out_ref[rows - RAD :],
        inner_ref,
        outer_ref,
    )


def edge_shapes(field):
    return [jax.ShapeDtypeStruct((RAD,) + field.shape[1:], bf16)] * 2


def first_call(support, owner, here, split, field, footprints, pieces):
    rows, frames, cols = field.shape
    tiles, slots, pixels, block = footprints.shape
    tile = cols // tiles
    chunks = rows // ROW_STEP
    return pl.pallas_call(
        functools.partial(first_kernel, tile, len(pieces)),
        name="first",
        in_specs=[smem, smem, smem, vmem, anywhere, anywhere] + [vmem] * len(pieces),
        out_specs=[vmem] * 3,
        out_shape=[jax.ShapeDtypeStruct(field.shape, bf16)] + edge_shapes(field),
        scratch_shapes=[
            pltpu.VMEM((chunks, tiles, slots, ROW_STEP * tile, block), bf16),
            pltpu.VMEM((chunks, ROW_STEP, frames, cols), bf16),
            pltpu.VMEM((tiles * slots // 2, frames, 2 * block), bf16),
            pltpu.SemaphoreType.DMA((chunks, tiles)),
            pltpu.SemaphoreType.DMA((chunks,)),
        ],
        compiler_params=pltpu.CompilerParams(vmem_limit_bytes=FIRST_VMEM * MIB),
    )(support, owner, here, split, field, footprints, *pieces)


def final_kernel(tile, tile_count, support_ref, owner_ref, here_ref, third_ref, prints_ref, *refs):
    old, new = refs[:tile_count], refs[tile_count : 2 * tile_count]
    out_ref, prints_buf, out_buf, lhs_ref, prints_sem, out_sem = refs[2 * tile_count :]
    frames = third_ref.shape[1]
    copies = chunk_copies(tile, prints_ref, prints_buf, prints_sem)
    results = [
        pltpu.make_async_copy(
            out_buf.at[c], out_ref.at[pl.ds(c * ROW_STEP, ROW_STEP)], out_sem.at[c]
        )
        for c in range(len(copies))
    ]
    for c in range(AHEAD):
        copies[c].start()
    gather_lhs(support_ref, owner_ref, here_ref, (old, new), lhs_ref)
    for c in range(len(copies)):
        copies[c].wait()
        if c + AHEAD < len(copies):
            copies[c + AHEAD].start()
        images = neural_rows(lhs_ref, prints_buf.at[c])
        images = [im[:frames] - im[frames:] for im in images]

        def finish(row, image):
            value = third_ref[c * ROW_STEP + row].astype(f32) + image
            out_buf[c, row] = value.astype(bf16)

        image_rows(tile, images, finish)
        results[c].start()
    for r in results:
        r.wait()


def final_call(support, owner, here, third, footprints, old, new):
    rows, frames, cols = third.shape
    tiles, slots, pixels, block = footprints.shape
    tile = cols // tiles
    chunks = rows // ROW_STEP
    return pl.pallas_call(
        functools.partial(final_kernel, tile, len(old)),
        name="final",
        in_specs=[smem, smem, smem, vmem, anywhere] + [vmem] * (2 * len(old)),
        out_specs=anywhere,
        out_shape=jax.ShapeDtypeStruct(third.shape, bf16),
        scratch_shapes=[
            pltpu.VMEM((chunks, tiles, slots, ROW_STEP * tile, block), bf16),
            pltpu.VMEM((chunks, ROW_STEP, frames, cols), bf16),
            pltpu.VMEM((tiles * slots // 2, 2 * frames, 2 * block), bf16),
            pltpu.SemaphoreType.DMA((chunks, tiles)),
            pltpu.SemaphoreType.DMA((chunks,)),
        ],
        compiler_params=pltpu.CompilerParams(vmem_limit_bytes=FINAL_VMEM * MIB),
    )(support, owner, here, third, footprints, *old, *new)


def tree_sum(terms):
    while len(terms) > 1:
        pairs = [a + b for a, b in zip(terms[::2], terms[1::2])]
        terms = pairs + terms[len(terms) - len(terms) % 2 :]
    return terms[0]


def cycle_pass(
    offsets_ref, here_ref, starts_ref, inner_ref, outer_ref, field_ref, weights_ref, out_ref,
    moved_ref, ready,
):
    rows, frames, cols = field_ref.shape
    extended = rows + 2 * RAD
    taps = weights_ref.shape[0]
    odd = here_ref[0] % 2 == 1
    width = cols // 2

    for j in range(taps):
        starts_ref[j] = (offsets_ref[1, j] + RAD) * extended + offsets_ref[0, j] + RAD
    sublanes = weights_ref.shape[2]
    shifts = range(-RAD, RAD + 1)

    def place_row(value, row, shifts, cache):
        sides = (value[:, :width], value[:, width:])

        def turned(p, m):
            if (p, m) not in cache:
                cache[p, m] = sides[p] if m == 0 else pltpu.roll(sides[p], (-m) % width, 1)
            return cache[p, m]

        for d in shifts:
            ends = [turned((p + d) % 2, (p + d) // 2) for p in range(2)]
            moved_ref[(d + RAD) * extended + row] = jnp.concatenate(ends, axis=1)

    def above(r):
        return jnp.where(odd, outer_ref[r], inner_ref[r])

    def below(r):
        return jnp.where(odd, inner_ref[r], outer_ref[r])

    def fill(source, count, base):
        def step(r, carry):
            place_row(source(r), base + r, shifts, {})
            return carry

        lax.fori_loop(0, count, step, 0)

    fill(lambda r: field_ref[r], RAD + 1, RAD)
    fill(above, RAD, 0)
    ready()
    groups = -(-taps // TAP_GROUP)
    span = frames // FRAME_PARTS
    parts = groups * FRAME_PARTS

    def sweep(first, count, source):
        def row_step(i, carry):
            y = first + i
            cache = {}
            value = None if source is None else source(i)
            for f in range(FRAME_PARTS):
                cut = slice(f * span, (f + 1) * span)
                total = jnp.zeros((span, cols), f32)
                for g in range(groups):
                    terms = []
                    for j in range(g * TAP_GROUP, min((g + 1) * TAP_GROUP, taps)):
                        weight = jnp.concatenate([weights_ref[j, y]] * (span // sublanes), axis=0)
                        terms.append(moved_ref[starts_ref[j] + y, cut, :] * weight)
                    total = total + tree_sum(terms).astype(f32)
                    if source is not None:
                        at = f * groups + g
                        part = shifts[at * len(shifts) // parts : (at + 1) * len(shifts) // parts]
                        place_row(value, y + 2 * RAD + 1, part, cache)
                out_ref[y, cut, :] = (field_ref[y, cut, :].astype(f32) - total).astype(bf16)
            return carry

        lax.fori_loop(0, count, row_step, 0)

    sweep(0, rows - RAD - 1, lambda i: field_ref[i + RAD + 1])
    sweep(rows - RAD - 1, RAD, below)
    sweep(rows - 1, 1, None)


def cycle_kernel(
    offsets_ref, here_ref, inner_ref, outer_ref, field_ref, weights_ref, out_ref, inner_out, outer_out,
    starts_ref, moved_ref, weights_buf, weights_sem,
):
    copy = pltpu.make_async_copy(weights_ref, weights_buf, weights_sem)
    copy.start()
    cycle_pass(
        offsets_ref, here_ref, starts_ref, inner_ref, outer_ref, field_ref, weights_buf, out_ref,
        moved_ref, copy.wait,
    )
    rows = out_ref.shape[0]
    write_edges(
        here_ref[0] % 2,
        lambda: out_ref[:RAD],
        lambda: out_ref[rows - RAD :],
        inner_out,
        outer_out,
    )


def cycle_call(offsets, here, inner, outer, field, weights):
    rows, frames, cols = field.shape
    banks = 2 * RAD + 1
    return pl.pallas_call(
        cycle_kernel,
        name="cycle",
        in_specs=[smem, smem, vmem, vmem, vmem, anywhere],
        out_specs=[vmem] * 3,
        out_shape=[jax.ShapeDtypeStruct(field.shape, bf16)] + edge_shapes(field),
        scratch_shapes=[
            pltpu.SMEM((weights.shape[0],), jnp.int32),
            pltpu.VMEM((banks * (rows + 2 * RAD), frames, cols), bf16),
            pltpu.VMEM(weights.shape, bf16),
            pltpu.SemaphoreType.DMA,
        ],
        compiler_params=pltpu.CompilerParams(vmem_limit_bytes=40 * MIB),
    )(offsets, here, inner, outer, field, weights)


def halo_rows(inner, outer):
    peers = lax.axis_size("tile")
    crossing = [(i, i + 1) for i in range(1, peers - 1, 2)]
    within = [(i, i + 1) for i in range(0, peers - 1, 2)]
    both = [pairs + [(j, i) for i, j in pairs] for pairs in (crossing, within)]
    return lax.ppermute(inner, "tile", both[0]), lax.ppermute(outer, "tile", both[1])


def square_sum(values):
    pixels, block = values.shape
    cut = values.reshape(pixels // LANES, LANES, block)
    return jnp.sum(
        tree_sum([cut[i] * cut[i] for i in range(pixels // LANES)]).astype(f32),
        axis=0,
        keepdims=True,
    )


def norm_kernel(
    share, tile_count, support_ref, owner_ref, here_ref, prints_ref, keep_ref, send_ref,
    buf_ref, sem_ref, square_ref,
):
    tiles, slots, pixels, block = prints_ref.shape
    half = keep_ref.shape[0]
    positions = 2 * half
    copies = [
        pltpu.make_async_copy(prints_ref.at[t], buf_ref.at[t], sem_ref.at[t]) for t in range(tiles)
    ]
    for c in copies:
        c.start()
    square_ref[...] = jnp.zeros_like(square_ref)
    for t in range(tiles):
        copies[t].wait()
        for k in range(0, slots, 2):
            pair = jnp.concatenate([buf_ref[t, k + i] for i in range(2)], axis=1)
            sums = square_sum(pair)
            for i in range(2):
                position = slot_position(support_ref, owner_ref, t * slots + k + i)
                place = place_of(jnp.maximum(position, 0), here_ref[0], tile_count, share)
                place = jnp.where(position >= 0, place, positions)
                square_ref[pl.ds(place, 1), :] += sums[:, i * block : (i + 1) * block]
    keep_ref[...] = square_ref[:half]
    squares = square_ref[half:positions]
    high = squares.astype(bf16)
    send_ref[:half] = high
    send_ref[half:] = (squares - high.astype(f32)).astype(bf16)


def norm_call(support, owner, here, footprints, tile_count):
    tiles, slots, pixels, block = footprints.shape
    positions = owner.shape[0]
    half = positions // 2
    return pl.pallas_call(
        functools.partial(norm_kernel, positions // tile_count, tile_count),
        name="norms",
        in_specs=[smem, smem, smem, anywhere],
        out_specs=[vmem] * 2,
        out_shape=[
            jax.ShapeDtypeStruct((half, block), f32),
            jax.ShapeDtypeStruct((2 * half, block), bf16),
        ],
        scratch_shapes=[
            pltpu.VMEM(footprints.shape, bf16),
            pltpu.SemaphoreType.DMA((tiles,)),
            pltpu.VMEM((positions + 8, block), f32),
        ],
        compiler_params=pltpu.CompilerParams(vmem_limit_bytes=FIRST_VMEM * MIB),
    )(support, owner, here, footprints)


def project_kernel(
    tile, tile_count, support_ref, owner_ref, offsets_ref, here_ref, join_ref, inner_ref, outer_ref,
    field_ref, norms_ref, weights_ref, prints_ref, whole_ref, keep_ref, send_ref,
    starts_ref, moved_ref, weights_buf, weights_sem, prints_buf, prints_sem, third_ref, lhs_ref, sum_ref,
):
    rows, frames, cols = field_ref.shape
    tiles, slots, pixels, block = prints_ref.shape
    group = LANES // tile
    half = keep_ref.shape[0]
    weights_copy = pltpu.make_async_copy(weights_ref, weights_buf, weights_sem)
    weights_copy.start()
    copies = [
        pltpu.make_async_copy(prints_ref.at[t], prints_buf.at[t], prints_sem.at[t])
        for t in range(tiles)
    ]
    for c in copies:
        c.start()
    sum_ref[...] = jnp.zeros_like(sum_ref)
    cycle_pass(
        offsets_ref, here_ref, starts_ref, inner_ref, outer_ref, field_ref, weights_buf, third_ref,
        moved_ref, weights_copy.wait,
    )
    positions = sum_ref.shape[0] - 1
    for h in range(rows // group):
        whole = []
        for r in range(group):
            row = h * group + r
            value = lax.dot_general(
                third_ref[row], join_ref[...], NN, preferred_element_type=f32
            )
            whole.append(value.astype(bf16))
            whole_ref[row] = whole[-1]
        for g in range(cols // LANES):
            cut = [w[:, g * LANES : (g + 1) * LANES] for w in whole]
            for t, part in enumerate(swap_groups(cut, tile)):
                lhs_ref[g * group + t, :, h * LANES : (h + 1) * LANES] = part
    for t in range(tiles):
        copies[t].wait()
        lhs = lhs_ref[t]
        for k in range(0, slots, 2):
            rhs = jnp.concatenate([prints_buf[t, k + i] for i in range(2)], axis=1)
            out = lax.dot_general(lhs, rhs, NN, preferred_element_type=f32)
            for i in range(2):
                position = slot_position(support_ref, owner_ref, t * slots + k + i)
                place = place_of(
                    jnp.maximum(position, 0), here_ref[0], tile_count, positions // tile_count
                )
                place = jnp.where(position >= 0, place, positions)
                sum_ref[place] += out[:, i * block : (i + 1) * block]
    keep_ref[...] = sum_ref[:half]
    send_ref[: half * frames] = sum_ref[half : 2 * half].reshape(half * frames, block).astype(bf16)
    send_ref[half * frames :] = norms_ref[...]


def project_call(
    support, owner, offsets, here, join, inner, outer, field, norms, weights, footprints, tile_count
):
    rows, frames, cols = field.shape
    tiles, slots, pixels, block = footprints.shape
    tile = cols // tiles
    positions = owner.shape[0]
    half = positions // 2
    banks = 2 * RAD + 1
    return pl.pallas_call(
        functools.partial(project_kernel, tile, tile_count),
        name="project",
        in_specs=[smem, smem, smem, smem, vmem, vmem, vmem, vmem, vmem, anywhere, anywhere],
        out_specs=[vmem] * 3,
        out_shape=[
            jax.ShapeDtypeStruct(field.shape, bf16),
            jax.ShapeDtypeStruct((half, frames, block), f32),
            jax.ShapeDtypeStruct((half * (frames + 2), block), bf16),
        ],
        scratch_shapes=[
            pltpu.SMEM((weights.shape[0],), jnp.int32),
            pltpu.VMEM((banks * (rows + 2 * RAD), frames, cols), bf16),
            pltpu.VMEM(weights.shape, bf16),
            pltpu.SemaphoreType.DMA,
            pltpu.VMEM(footprints.shape, bf16),
            pltpu.SemaphoreType.DMA((tiles,)),
            pltpu.VMEM(field.shape, bf16),
            pltpu.VMEM((tiles, frames, pixels), bf16),
            pltpu.VMEM((positions + 1, frames, block), f32),
        ],
        compiler_params=pltpu.CompilerParams(vmem_limit_bytes=52 * MIB),
    )(support, owner, offsets, here, join, inner, outer, field, norms, weights, footprints)


def gathered(value):
    peers = lax.axis_size("tile")
    pieces = {0: value}
    step = peers // 2
    while step >= 1:
        pairs = [(i, i ^ step) for i in range(peers)]
        for apart in sorted(pieces):
            pieces[apart ^ step] = lax.ppermute(pieces[apart], "tile", pairs)
        step //= 2
    return [pieces[apart] for apart in range(peers)]


def reduced(keep, norms, send):
    peers = lax.axis_size("tile")
    step = 1
    while True:
        half, frames, block = keep.shape
        arrived = lax.ppermute(send, "tile", [(i, i ^ step) for i in range(peers)]).astype(f32)
        keep = keep + arrived[: half * frames].reshape(keep.shape)
        norms = norms + arrived[half * frames : -half] + arrived[-half:]
        step *= 2
        if step == peers:
            return keep, norms
        half = half // 2
        high = norms[half:].astype(bf16)
        low = (norms[half:] - high.astype(f32)).astype(bf16)
        send = jnp.concatenate([keep[half:].astype(bf16).reshape(half * frames, block), high, low])
        keep, norms = keep[:half], norms[:half]


def filter_kernel(odd_ref, taps_ref, own_ref, even_ref, other_ref, out_ref):
    count, frames, block = own_ref.shape
    width = taps_ref.shape[1]
    base = jnp.broadcast_to(taps_ref[...], (frames, width))
    band = pltpu.roll(base, 0, 1, stride=1, stride_axis=0)
    before, here, after = (band[:, i * frames : (i + 1) * frames] for i in range(3))
    odd = odd_ref[0] == 1
    first = jnp.where(odd, before, after)
    second = jnp.where(odd, after, before)
    for q in range(count):
        out = lax.dot_general(here, own_ref[q], NN, precision=highest, preferred_element_type=f32)
        out += lax.dot_general(
            first, even_ref[q].astype(f32), NN, precision=highest, preferred_element_type=f32
        )
        out += lax.dot_general(
            second, other_ref[q].astype(f32), NN, precision=highest, preferred_element_type=f32
        )
        out_ref[q] = jnp.maximum(out, 0.0).astype(bf16)


def filter_call(odd, taps, own, even, other):
    frames = own.shape[1]
    reach = taps.shape[0]
    half = (reach - 1) // 2
    width = 4 * frames
    lead = frames - half
    line = jnp.pad(taps[::-1], (lead, width - reach - lead)).reshape(1, width)
    return pl.pallas_call(
        filter_kernel,
        name="wiener",
        in_specs=[smem, vmem, vmem, vmem, vmem],
        out_specs=vmem,
        out_shape=jax.ShapeDtypeStruct(own.shape, bf16),
        compiler_params=pltpu.CompilerParams(vmem_limit_bytes=16 * MIB),
    )(odd, line, own, even, other)


def body(movie, footprints, support, cycle_offsets, cycle_weights, owner_map, traces_old, taps):
    tile_count, time_count = lax.axis_size("tile"), lax.axis_size("tm")
    tile_here, time_here = lax.axis_index("tile"), lax.axis_index("tm")
    rows, cols, frames = movie.shape
    tiles, slots, tile, _, block = footprints.shape
    positions = owner_map.shape[0]
    share = positions // tile_count
    owned = traces_old.shape[0]
    prints = footprints.reshape(tiles, slots, tile * tile, block)

    field = movie.transpose(0, 2, 1)
    columns = jnp.arange(cols, dtype=jnp.int32)
    source = 2 * (columns % (cols // 2)) + columns // (cols // 2)
    split = (columns[:, None] == source[None, :]).astype(bf16)
    join = (source[:, None] == columns[None, :]).astype(bf16)
    reached = columns[None, :] + cycle_offsets[:, 1:2]
    inside = (reached >= 0) & (reached < cols)
    weights = jnp.where(inside[:, None, :], cycle_weights, 0.0).astype(bf16)
    weights = lax.dot_general(
        weights, split, (((2,), (0,)), ((), ())), preferred_element_type=f32
    ).astype(bf16)
    offsets, slots_held = cycle_offsets.T, support.T
    here = tile_here.astype(jnp.int32).reshape(1)

    outgoing = traces_old.T.reshape(time_count, frames, owned)
    group_old = lax.all_to_all(outgoing, "tm", split_axis=0, concat_axis=0, tiled=True)
    pieces = block // owned
    group_old = group_old.reshape(share, pieces, frames, owned).transpose(0, 2, 1, 3)
    group_old = group_old.reshape(share, frames, block)
    group_old, weights = lax.optimization_barrier((group_old, weights))
    old = gathered(group_old)

    first_res, inner, outer = first_call(slots_held, owner_map, here, split, field, prints, old)
    inner, weights = lax.optimization_barrier((inner, weights))
    inner, outer = halo_rows(inner, outer)
    weights = jnp.broadcast_to(weights[:, :, None, :], weights.shape[:2] + (8, cols))
    inner, outer, weights = lax.optimization_barrier((inner, outer, weights))
    second_res, inner, outer = cycle_call(offsets, here, inner, outer, first_res, weights)
    inner, tied = lax.optimization_barrier((inner, prints))
    inner, outer = halo_rows(inner, outer)
    norms, norms_away = norm_call(slots_held, owner_map, here, tied, tile_count)
    inner, outer, norms_away = lax.optimization_barrier((inner, outer, norms_away))
    third_res, keep, send = project_call(
        slots_held, owner_map, offsets, here, join, inner, outer, second_res, norms_away, weights,
        prints, tile_count,
    )
    total, norms = reduced(keep, norms, send)

    update = group_old.astype(f32) + total / (norms[:, None, :] + ridge_term)
    narrow = update.astype(bf16)
    even_pairs = [(i, i ^ 1) for i in range(time_count)]
    odd_pairs = [(i, i + 1) for i in range(1, time_count - 1, 2)]
    odd_pairs = odd_pairs + [(j, i) for i, j in odd_pairs]
    even = lax.ppermute(narrow, "tm", even_pairs)
    other = lax.ppermute(narrow, "tm", odd_pairs)
    parity = (time_here % 2).astype(jnp.int32).reshape(1)
    fresh = filter_call(parity, taps, update, even, other)

    new = gathered(fresh)
    leaving = fresh.reshape(share, frames, pieces, owned).transpose(0, 2, 1, 3)
    leaving = leaving.reshape(time_count, frames, owned)
    owner_new = lax.all_to_all(leaving, "tm", split_axis=0, concat_axis=0, tiled=True)
    residual = final_call(slots_held, owner_map, here, third_res, prints, old, new)
    residual, owner_new = lax.optimization_barrier((residual, owner_new))
    traces_new = owner_new.reshape(time_count * frames, owned).T
    return residual.transpose(0, 2, 1), traces_new


def solution(mesh):
    return jax.shard_map(
        body,
        mesh=mesh,
        in_specs=(
            P("tile", None, "tm"),
            P("tile", None, None, None, None),
            P("tile", None),
            P(),
            P(None, "tile", None),
            P(),
            P(("tile", "tm"), None),
            P(),
        ),
        out_specs=(P("tile", None, "tm"), P(("tile", "tm"), None)),
        check_vma=False,
    )
```

```python
import functools

import jax
import jax.numpy as jnp
from jax import lax
from jax.experimental import pallas as pl
from jax.experimental.pallas import tpu as pltpu
from jax.sharding import PartitionSpec as P

RAD = 8
LANES = 128
ROW_STEP = 8
AHEAD = 2
FIRST_VMEM = 53
FINAL_VMEM = 53
TAP_GROUP = 4
MIB = 1024 * 1024
FRAME_PARTS = 2
ridge_term = 1.0
highest = lax.Precision.HIGHEST
bf16 = jnp.bfloat16
f32 = jnp.float32
NT = (((1,), (1,)), ((), ()))
NN = (((1,), (0,)), ((), ()))

smem = pl.BlockSpec(memory_space=pltpu.SMEM)
vmem = pl.BlockSpec(memory_space=pltpu.VMEM)
anywhere = pl.BlockSpec(memory_space=pl.ANY)


def swap_groups(parts, width):
    count = len(parts)
    lane = lax.broadcasted_iota(jnp.int32, parts[0].shape, 1)
    dist = count // 2
    while dist >= 1:
        upper = (lane // (width * dist)) % 2 == 1
        out = list(parts)
        for a in range(count):
            if a & dist:
                continue
            low, high = parts[a], parts[a | dist]
            out[a] = jnp.where(upper, pltpu.roll(high, width * dist, 1), low)
            out[a | dist] = jnp.where(upper, high, pltpu.roll(low, LANES - width * dist, 1))
        parts = out
        dist //= 2
    return parts


def slot_position(support_ref, owner_ref, slot):
    slots = support_ref.shape[0]
    block = support_ref[slot % slots, slot // slots]
    return jnp.where(block >= 0, owner_ref[jnp.maximum(block, 0)], -1)


def place_of(position, here, tile_count, share):
    apart = (position // share) ^ here
    bits = tile_count.bit_length() - 1
    rank = sum(((apart >> b) & 1) << (bits - 1 - b) for b in range(bits))
    return rank * share + position % share


def gather_lhs(support_ref, owner_ref, here_ref, pieces, lhs_ref):
    tile_count = len(pieces[0])
    share = pieces[0][0].shape[0]
    for slot in range(2 * lhs_ref.shape[0]):
        position = slot_position(support_ref, owner_ref, slot)
        live = position >= 0
        index = jnp.maximum(position, 0)
        apart = (index // share) ^ here_ref[0]
        row = index % share
        parts = []
        for refs in pieces:
            value = refs[0][row]
            for rank in range(1, tile_count):
                value = jnp.where(apart == rank, refs[rank][row], value)
            parts.append(jnp.where(live, value, jnp.zeros_like(value)))
        value = parts[0] if len(parts) == 1 else jnp.concatenate(parts, axis=0)
        block = value.shape[1]
        lhs_ref[slot // 2, :, (slot % 2) * block : (slot % 2 + 1) * block] = value


def neural_rows(lhs_ref, chunk_ref):
    tiles, slots = chunk_ref.shape[:2]
    images = []
    for t in range(tiles):
        image = None
        for k in range(0, slots, 2):
            rhs = jnp.concatenate([chunk_ref[t, k + i] for i in range(2)], axis=1)
            part = lax.dot_general(
                lhs_ref[(t * slots + k) // 2], rhs, NT, preferred_element_type=f32
            )
            image = part if image is None else image + part
        images.append(image)
    return images


class Copies:
    def __init__(self, parts):
        self.parts = parts

    def start(self):
        for part in self.parts:
            part.start()

    def wait(self):
        for part in self.parts:
            part.wait()


def chunk_copies(tile, prints_ref, chunks_ref, sems):
    size = ROW_STEP * tile
    return [
        Copies(
            [
                pltpu.make_async_copy(
                    prints_ref.at[t, :, pl.ds(c * size, size), :], chunks_ref.at[c, t], sems.at[c, t]
                )
                for t in range(chunks_ref.shape[1])
            ]
        )
        for c in range(chunks_ref.shape[0])
    ]


def field_copies(field_ref, chunks_ref, sems):
    return [
        pltpu.make_async_copy(
            field_ref.at[pl.ds(c * ROW_STEP, ROW_STEP)], chunks_ref.at[c], sems.at[c]
        )
        for c in range(chunks_ref.shape[0])
    ]


def image_rows(tile, images, finish):
    group = LANES // tile
    for h in range(ROW_STEP // group):
        sides = []
        for g in range(0, len(images), group):
            cut = [im[:, h * LANES : (h + 1) * LANES] for im in images[g : g + group]]
            sides.append(swap_groups(cut, tile))
        for r in range(group):
            finish(h * group + r, jnp.concatenate([side[r] for side in sides], axis=1))


def write_edges(odd, first_rows, last_rows, inner_ref, outer_ref):
    @pl.when(odd == 1)
    def _():
        inner_ref[...] = last_rows()
        outer_ref[...] = first_rows()

    @pl.when(odd != 1)
    def _():
        inner_ref[...] = first_rows()
        outer_ref[...] = last_rows()


def first_kernel(tile, tile_count, support_ref, owner_ref, here_ref, split_ref, movie_ref, prints_ref, *refs):
    pieces = refs[:tile_count]
    out_ref, inner_ref, outer_ref, prints_buf, movie_buf, lhs_ref, prints_sem, movie_sem = refs[tile_count:]
    copies = chunk_copies(tile, prints_ref, prints_buf, prints_sem)
    movies = field_copies(movie_ref, movie_buf, movie_sem)
    for c in range(AHEAD):
        movies[c].start()
        copies[c].start()
    gather_lhs(support_ref, owner_ref, here_ref, (pieces,), lhs_ref)
    for c in range(len(copies)):
        movies[c].wait()
        copies[c].wait()
        if c + AHEAD < len(copies):
            movies[c + AHEAD].start()
            copies[c + AHEAD].start()
        images = neural_rows(lhs_ref, prints_buf.at[c])

        def finish(row, image):
            value = (movie_buf[c, row].astype(f32) - image).astype(bf16)
            moved = lax.dot_general(value, split_ref[...], NN, preferred_element_type=f32)
            out_ref[c * ROW_STEP + row] = moved.astype(bf16)

        image_rows(tile, images, finish)
    rows = out_ref.shape[0]
    write_edges(
        here_ref[0] % 2,
        lambda: out_ref[:RAD],
        lambda: out_ref[rows - RAD :],
        inner_ref,
        outer_ref,
    )


def edge_shapes(field):
    return [jax.ShapeDtypeStruct((RAD,) + field.shape[1:], bf16)] * 2


def first_call(support, owner, here, split, field, footprints, pieces):
    rows, frames, cols = field.shape
    tiles, slots, pixels, block = footprints.shape
    tile = cols // tiles
    chunks = rows // ROW_STEP
    return pl.pallas_call(
        functools.partial(first_kernel, tile, len(pieces)),
        name="first",
        in_specs=[smem, smem, smem, vmem, anywhere, anywhere] + [vmem] * len(pieces),
        out_specs=[vmem] * 3,
        out_shape=[jax.ShapeDtypeStruct(field.shape, bf16)] + edge_shapes(field),
        scratch_shapes=[
            pltpu.VMEM((chunks, tiles, slots, ROW_STEP * tile, block), bf16),
            pltpu.VMEM((chunks, ROW_STEP, frames, cols), bf16),
            pltpu.VMEM((tiles * slots // 2, frames, 2 * block), bf16),
            pltpu.SemaphoreType.DMA((chunks, tiles)),
            pltpu.SemaphoreType.DMA((chunks,)),
        ],
        compiler_params=pltpu.CompilerParams(vmem_limit_bytes=FIRST_VMEM * MIB),
    )(support, owner, here, split, field, footprints, *pieces)


def final_kernel(tile, tile_count, support_ref, owner_ref, here_ref, third_ref, prints_ref, *refs):
    old, new = refs[:tile_count], refs[tile_count : 2 * tile_count]
    out_ref, prints_buf, out_buf, lhs_ref, prints_sem, out_sem = refs[2 * tile_count :]
    frames = third_ref.shape[1]
    copies = chunk_copies(tile, prints_ref, prints_buf, prints_sem)
    results = [
        pltpu.make_async_copy(
            out_buf.at[c], out_ref.at[pl.ds(c * ROW_STEP, ROW_STEP)], out_sem.at[c]
        )
        for c in range(len(copies))
    ]
    for c in range(AHEAD):
        copies[c].start()
    gather_lhs(support_ref, owner_ref, here_ref, (old, new), lhs_ref)
    for c in range(len(copies)):
        copies[c].wait()
        if c + AHEAD < len(copies):
            copies[c + AHEAD].start()
        images = neural_rows(lhs_ref, prints_buf.at[c])
        images = [im[:frames] - im[frames:] for im in images]

        def finish(row, image):
            value = third_ref[c * ROW_STEP + row].astype(f32) + image
            out_buf[c, row] = value.astype(bf16)

        image_rows(tile, images, finish)
        results[c].start()
    for r in results:
        r.wait()


def final_call(support, owner, here, third, footprints, old, new):
    rows, frames, cols = third.shape
    tiles, slots, pixels, block = footprints.shape
    tile = cols // tiles
    chunks = rows // ROW_STEP
    return pl.pallas_call(
        functools.partial(final_kernel, tile, len(old)),
        name="final",
        in_specs=[smem, smem, smem, vmem, anywhere] + [vmem] * (2 * len(old)),
        out_specs=anywhere,
        out_shape=jax.ShapeDtypeStruct(third.shape, bf16),
        scratch_shapes=[
            pltpu.VMEM((chunks, tiles, slots, ROW_STEP * tile, block), bf16),
            pltpu.VMEM((chunks, ROW_STEP, frames, cols), bf16),
            pltpu.VMEM((tiles * slots // 2, 2 * frames, 2 * block), bf16),
            pltpu.SemaphoreType.DMA((chunks, tiles)),
            pltpu.SemaphoreType.DMA((chunks,)),
        ],
        compiler_params=pltpu.CompilerParams(vmem_limit_bytes=FINAL_VMEM * MIB),
    )(support, owner, here, third, footprints, *old, *new)


def tree_sum(terms):
    while len(terms) > 1:
        pairs = [a + b for a, b in zip(terms[::2], terms[1::2])]
        terms = pairs + terms[len(terms) - len(terms) % 2 :]
    return terms[0]


def cycle_pass(
    offsets_ref, here_ref, starts_ref, inner_ref, outer_ref, field_ref, weights_ref, out_ref,
    moved_ref, ready,
):
    rows, frames, cols = field_ref.shape
    extended = rows + 2 * RAD
    taps = weights_ref.shape[0]
    odd = here_ref[0] % 2 == 1
    width = cols // 2

    for j in range(taps):
        starts_ref[j] = (offsets_ref[1, j] + RAD) * extended + offsets_ref[0, j] + RAD
    sublanes = weights_ref.shape[2]
    shifts = range(-RAD, RAD + 1)

    def place_row(value, row, shifts, cache):
        sides = (value[:, :width], value[:, width:])

        def turned(p, m):
            if (p, m) not in cache:
                cache[p, m] = sides[p] if m == 0 else pltpu.roll(sides[p], (-m) % width, 1)
            return cache[p, m]

        for d in shifts:
            ends = [turned((p + d) % 2, (p + d) // 2) for p in range(2)]
            moved_ref[(d + RAD) * extended + row] = jnp.concatenate(ends, axis=1)

    def above(r):
        return jnp.where(odd, outer_ref[r], inner_ref[r])

    def below(r):
        return jnp.where(odd, inner_ref[r], outer_ref[r])

    def fill(source, count, base):
        def step(r, carry):
            place_row(source(r), base + r, shifts, {})
            return carry

        lax.fori_loop(0, count, step, 0)

    fill(lambda r: field_ref[r], RAD + 1, RAD)
    fill(above, RAD, 0)
    ready()
    groups = -(-taps // TAP_GROUP)
    span = frames // FRAME_PARTS
    parts = groups * FRAME_PARTS

    def sweep(first, count, source):
        def row_step(i, carry):
            y = first + i
            cache = {}
            value = None if source is None else source(i)
            for f in range(FRAME_PARTS):
                cut = slice(f * span, (f + 1) * span)
                total = jnp.zeros((span, cols), f32)
                for g in range(groups):
                    terms = []
                    for j in range(g * TAP_GROUP, min((g + 1) * TAP_GROUP, taps)):
                        weight = jnp.concatenate([weights_ref[j, y]] * (span // sublanes), axis=0)
                        terms.append(moved_ref[starts_ref[j] + y, cut, :] * weight)
                    total = total + tree_sum(terms).astype(f32)
                    if source is not None:
                        at = f * groups + g
                        part = shifts[at * len(shifts) // parts : (at + 1) * len(shifts) // parts]
                        place_row(value, y + 2 * RAD + 1, part, cache)
                out_ref[y, cut, :] = (field_ref[y, cut, :].astype(f32) - total).astype(bf16)
            return carry

        lax.fori_loop(0, count, row_step, 0)

    sweep(0, rows - RAD - 1, lambda i: field_ref[i + RAD + 1])
    sweep(rows - RAD - 1, RAD, below)
    sweep(rows - 1, 1, None)


def cycle_kernel(
    offsets_ref, here_ref, inner_ref, outer_ref, field_ref, weights_ref, out_ref, inner_out, outer_out,
    starts_ref, moved_ref, weights_buf, weights_sem,
):
    copy = pltpu.make_async_copy(weights_ref, weights_buf, weights_sem)
    copy.start()
    cycle_pass(
        offsets_ref, here_ref, starts_ref, inner_ref, outer_ref, field_ref, weights_buf, out_ref,
        moved_ref, copy.wait,
    )
    rows = out_ref.shape[0]
    write_edges(
        here_ref[0] % 2,
        lambda: out_ref[:RAD],
        lambda: out_ref[rows - RAD :],
        inner_out,
        outer_out,
    )


def cycle_call(offsets, here, inner, outer, field, weights):
    rows, frames, cols = field.shape
    banks = 2 * RAD + 1
    return pl.pallas_call(
        cycle_kernel,
        name="cycle",
        in_specs=[smem, smem, vmem, vmem, vmem, anywhere],
        out_specs=[vmem] * 3,
        out_shape=[jax.ShapeDtypeStruct(field.shape, bf16)] + edge_shapes(field),
        scratch_shapes=[
            pltpu.SMEM((weights.shape[0],), jnp.int32),
            pltpu.VMEM((banks * (rows + 2 * RAD), frames, cols), bf16),
            pltpu.VMEM(weights.shape, bf16),
            pltpu.SemaphoreType.DMA,
        ],
        compiler_params=pltpu.CompilerParams(vmem_limit_bytes=40 * MIB),
    )(offsets, here, inner, outer, field, weights)


def spread_kernel(weights_ref, out_ref):
    taps, rows, sublanes, cols = out_ref.shape

    def step(y, carry):
        for j in range(taps):
            row = jnp.broadcast_to(weights_ref[j, pl.ds(y, 1), :], (sublanes, cols))
            out_ref[j, y] = row.astype(bf16)
        return carry

    lax.fori_loop(0, rows, step, 0)


def spread_call(weights):
    shape = weights.shape[:2] + (8,) + weights.shape[2:]
    return pl.pallas_call(
        spread_kernel,
        name="spread",
        in_specs=[vmem],
        out_specs=vmem,
        out_shape=jax.ShapeDtypeStruct(shape, bf16),
        compiler_params=pltpu.CompilerParams(vmem_limit_bytes=2 * MIB),
    )(weights)


def halo_rows(inner, outer):
    peers = lax.axis_size("tile")
    crossing = [(i, i + 1) for i in range(1, peers - 1, 2)]
    within = [(i, i + 1) for i in range(0, peers - 1, 2)]
    both = [pairs + [(j, i) for i, j in pairs] for pairs in (crossing, within)]
    return lax.ppermute(inner, "tile", both[0]), lax.ppermute(outer, "tile", both[1])


def square_sum(values):
    pixels, block = values.shape
    cut = values.reshape(pixels // LANES, LANES, block)
    return jnp.sum(
        tree_sum([cut[i] * cut[i] for i in range(pixels // LANES)]).astype(f32),
        axis=0,
        keepdims=True,
    )


def norm_kernel(
    share, tile_count, support_ref, owner_ref, here_ref, prints_ref, keep_ref, send_ref,
    buf_ref, sem_ref, square_ref,
):
    tiles, slots, pixels, block = prints_ref.shape
    half = keep_ref.shape[0]
    positions = 2 * half
    copies = [
        pltpu.make_async_copy(prints_ref.at[t], buf_ref.at[t], sem_ref.at[t]) for t in range(tiles)
    ]
    for c in copies:
        c.start()
    square_ref[...] = jnp.zeros_like(square_ref)
    for t in range(tiles):
        copies[t].wait()
        for k in range(0, slots, 2):
            pair = jnp.concatenate([buf_ref[t, k + i] for i in range(2)], axis=1)
            sums = square_sum(pair)
            for i in range(2):
                position = slot_position(support_ref, owner_ref, t * slots + k + i)
                place = place_of(jnp.maximum(position, 0), here_ref[0], tile_count, share)
                place = jnp.where(position >= 0, place, positions)
                square_ref[pl.ds(place, 1), :] += sums[:, i * block : (i + 1) * block]
    keep_ref[...] = square_ref[:half]
    squares = square_ref[half:positions]
    high = squares.astype(bf16)
    send_ref[:half] = high
    send_ref[half:] = (squares - high.astype(f32)).astype(bf16)


def norm_call(support, owner, here, footprints, tile_count):
    tiles, slots, pixels, block = footprints.shape
    positions = owner.shape[0]
    half = positions // 2
    return pl.pallas_call(
        functools.partial(norm_kernel, positions // tile_count, tile_count),
        name="norms",
        in_specs=[smem, smem, smem, anywhere],
        out_specs=[vmem] * 2,
        out_shape=[
            jax.ShapeDtypeStruct((half, block), f32),
            jax.ShapeDtypeStruct((2 * half, block), bf16),
        ],
        scratch_shapes=[
            pltpu.VMEM(footprints.shape, bf16),
            pltpu.SemaphoreType.DMA((tiles,)),
            pltpu.VMEM((positions + 8, block), f32),
        ],
        compiler_params=pltpu.CompilerParams(vmem_limit_bytes=FIRST_VMEM * MIB),
    )(support, owner, here, footprints)


def project_kernel(
    tile, tile_count, support_ref, owner_ref, offsets_ref, here_ref, join_ref, inner_ref, outer_ref,
    field_ref, norms_ref, weights_ref, prints_ref, whole_ref, keep_ref, send_ref,
    starts_ref, moved_ref, weights_buf, weights_sem, prints_buf, prints_sem, third_ref, lhs_ref, sum_ref,
):
    rows, frames, cols = field_ref.shape
    tiles, slots, pixels, block = prints_ref.shape
    group = LANES // tile
    half = keep_ref.shape[0]
    weights_copy = pltpu.make_async_copy(weights_ref, weights_buf, weights_sem)
    weights_copy.start()
    copies = [
        pltpu.make_async_copy(prints_ref.at[t], prints_buf.at[t], prints_sem.at[t])
        for t in range(tiles)
    ]
    for c in copies:
        c.start()
    sum_ref[...] = jnp.zeros_like(sum_ref)
    cycle_pass(
        offsets_ref, here_ref, starts_ref, inner_ref, outer_ref, field_ref, weights_buf, third_ref,
        moved_ref, weights_copy.wait,
    )
    positions = sum_ref.shape[0] - 1
    for h in range(rows // group):
        whole = []
        for r in range(group):
            row = h * group + r
            value = lax.dot_general(
                third_ref[row], join_ref[...], NN, preferred_element_type=f32
            )
            whole.append(value.astype(bf16))
            whole_ref[row] = whole[-1]
        for g in range(cols // LANES):
            cut = [w[:, g * LANES : (g + 1) * LANES] for w in whole]
            for t, part in enumerate(swap_groups(cut, tile)):
                lhs_ref[g * group + t, :, h * LANES : (h + 1) * LANES] = part
    for t in range(tiles):
        copies[t].wait()
        lhs = lhs_ref[t]
        for k in range(0, slots, 2):
            rhs = jnp.concatenate([prints_buf[t, k + i] for i in range(2)], axis=1)
            out = lax.dot_general(lhs, rhs, NN, preferred_element_type=f32)
            for i in range(2):
                position = slot_position(support_ref, owner_ref, t * slots + k + i)
                place = place_of(
                    jnp.maximum(position, 0), here_ref[0], tile_count, positions // tile_count
                )
                place = jnp.where(position >= 0, place, positions)
                sum_ref[place] += out[:, i * block : (i + 1) * block]
    keep_ref[...] = sum_ref[:half]
    send_ref[: half * frames] = sum_ref[half : 2 * half].reshape(half * frames, block).astype(bf16)
    send_ref[half * frames :] = norms_ref[...]


def project_call(
    support, owner, offsets, here, join, inner, outer, field, norms, weights, footprints, tile_count
):
    rows, frames, cols = field.shape
    tiles, slots, pixels, block = footprints.shape
    tile = cols // tiles
    positions = owner.shape[0]
    half = positions // 2
    banks = 2 * RAD + 1
    return pl.pallas_call(
        functools.partial(project_kernel, tile, tile_count),
        name="project",
        in_specs=[smem, smem, smem, smem, vmem, vmem, vmem, vmem, vmem, anywhere, anywhere],
        out_specs=[vmem] * 3,
        out_shape=[
            jax.ShapeDtypeStruct(field.shape, bf16),
            jax.ShapeDtypeStruct((half, frames, block), f32),
            jax.ShapeDtypeStruct((half * (frames + 2), block), bf16),
        ],
        scratch_shapes=[
            pltpu.SMEM((weights.shape[0],), jnp.int32),
            pltpu.VMEM((banks * (rows + 2 * RAD), frames, cols), bf16),
            pltpu.VMEM(weights.shape, bf16),
            pltpu.SemaphoreType.DMA,
            pltpu.VMEM(footprints.shape, bf16),
            pltpu.SemaphoreType.DMA((tiles,)),
            pltpu.VMEM(field.shape, bf16),
            pltpu.VMEM((tiles, frames, pixels), bf16),
            pltpu.VMEM((positions + 1, frames, block), f32),
        ],
        compiler_params=pltpu.CompilerParams(vmem_limit_bytes=52 * MIB),
    )(support, owner, offsets, here, join, inner, outer, field, norms, weights, footprints)


def gathered(value):
    peers = lax.axis_size("tile")
    pieces = {0: value}
    step = peers // 2
    while step >= 1:
        pairs = [(i, i ^ step) for i in range(peers)]
        for apart in sorted(pieces):
            pieces[apart ^ step] = lax.ppermute(pieces[apart], "tile", pairs)
        step //= 2
    return [pieces[apart] for apart in range(peers)]


def reduced(keep, norms, send):
    peers = lax.axis_size("tile")
    step = 1
    while True:
        half, frames, block = keep.shape
        arrived = lax.ppermute(send, "tile", [(i, i ^ step) for i in range(peers)]).astype(f32)
        keep = keep + arrived[: half * frames].reshape(keep.shape)
        norms = norms + arrived[half * frames : -half] + arrived[-half:]
        step *= 2
        if step == peers:
            return keep, norms
        half = half // 2
        high = norms[half:].astype(bf16)
        low = (norms[half:] - high.astype(f32)).astype(bf16)
        send = jnp.concatenate([keep[half:].astype(bf16).reshape(half * frames, block), high, low])
        keep, norms = keep[:half], norms[:half]


def filter_kernel(odd_ref, taps_ref, own_ref, even_ref, other_ref, out_ref):
    count, frames, block = own_ref.shape
    width = taps_ref.shape[1]
    base = jnp.broadcast_to(taps_ref[...], (frames, width))
    band = pltpu.roll(base, 0, 1, stride=1, stride_axis=0)
    before, here, after = (band[:, i * frames : (i + 1) * frames] for i in range(3))
    odd = odd_ref[0] == 1
    first = jnp.where(odd, before, after)
    second = jnp.where(odd, after, before)
    for q in range(count):
        out = lax.dot_general(here, own_ref[q], NN, precision=highest, preferred_element_type=f32)
        out += lax.dot_general(
            first, even_ref[q].astype(f32), NN, precision=highest, preferred_element_type=f32
        )
        out += lax.dot_general(
            second, other_ref[q].astype(f32), NN, precision=highest, preferred_element_type=f32
        )
        out_ref[q] = jnp.maximum(out, 0.0).astype(bf16)


def filter_call(odd, taps, own, even, other):
    frames = own.shape[1]
    reach = taps.shape[0]
    half = (reach - 1) // 2
    width = 4 * frames
    lead = frames - half
    line = jnp.pad(taps[::-1], (lead, width - reach - lead)).reshape(1, width)
    return pl.pallas_call(
        filter_kernel,
        name="wiener",
        in_specs=[smem, vmem, vmem, vmem, vmem],
        out_specs=vmem,
        out_shape=jax.ShapeDtypeStruct(own.shape, bf16),
        compiler_params=pltpu.CompilerParams(vmem_limit_bytes=16 * MIB),
    )(odd, line, own, even, other)


def body(movie, footprints, support, cycle_offsets, cycle_weights, owner_map, traces_old, taps):
    tile_count, time_count = lax.axis_size("tile"), lax.axis_size("tm")
    tile_here, time_here = lax.axis_index("tile"), lax.axis_index("tm")
    rows, cols, frames = movie.shape
    tiles, slots, tile, _, block = footprints.shape
    positions = owner_map.shape[0]
    share = positions // tile_count
    owned = traces_old.shape[0]
    prints = footprints.reshape(tiles, slots, tile * tile, block)

    field = movie.transpose(0, 2, 1)
    columns = jnp.arange(cols, dtype=jnp.int32)
    source = 2 * (columns % (cols // 2)) + columns // (cols // 2)
    split = (columns[:, None] == source[None, :]).astype(bf16)
    join = (source[:, None] == columns[None, :]).astype(bf16)
    reached = columns[None, :] + cycle_offsets[:, 1:2]
    inside = (reached >= 0) & (reached < cols)
    offsets, slots_held = cycle_offsets.T, support.T
    here = tile_here.astype(jnp.int32).reshape(1)

    outgoing = traces_old.T.reshape(time_count, frames, owned)
    group_old = lax.all_to_all(outgoing, "tm", split_axis=0, concat_axis=0, tiled=True)
    pieces = block // owned
    group_old = group_old.reshape(share, pieces, frames, owned).transpose(0, 2, 1, 3)
    group_old = group_old.reshape(share, frames, block)
    norms, norms_away = norm_call(slots_held, owner_map, here, prints, tile_count)
    group_old, norms_away = lax.optimization_barrier((group_old, norms_away))
    old = gathered(group_old)

    first_res, inner, outer = first_call(slots_held, owner_map, here, split, field, prints, old)
    inner, cycle_weights = lax.optimization_barrier((inner, cycle_weights))
    inner, outer = halo_rows(inner, outer)
    weights = jnp.where(inside[:, None, :], cycle_weights, 0.0).astype(bf16)
    weights = lax.dot_general(
        weights, split, (((2,), (0,)), ((), ())), preferred_element_type=f32
    )
    weights = spread_call(weights)
    inner, outer, weights = lax.optimization_barrier((inner, outer, weights))
    second_res, inner, outer = cycle_call(offsets, here, inner, outer, first_res, weights)
    inner, outer = halo_rows(inner, outer)
    third_res, keep, send = project_call(
        slots_held, owner_map, offsets, here, join, inner, outer, second_res, norms_away, weights,
        prints, tile_count,
    )
    total, norms = reduced(keep, norms, send)

    update = group_old.astype(f32) + total / (norms[:, None, :] + ridge_term)
    narrow = update.astype(bf16)
    even_pairs = [(i, i ^ 1) for i in range(time_count)]
    odd_pairs = [(i, i + 1) for i in range(1, time_count - 1, 2)]
    odd_pairs = odd_pairs + [(j, i) for i, j in odd_pairs]
    even = lax.ppermute(narrow, "tm", even_pairs)
    other = lax.ppermute(narrow, "tm", odd_pairs)
    parity = (time_here % 2).astype(jnp.int32).reshape(1)
    fresh = filter_call(parity, taps, update, even, other)

    new = gathered(fresh)
    leaving = fresh.reshape(share, frames, pieces, owned).transpose(0, 2, 1, 3)
    leaving = leaving.reshape(time_count, frames, owned)
    owner_new = lax.all_to_all(leaving, "tm", split_axis=0, concat_axis=0, tiled=True)
    residual = final_call(slots_held, owner_map, here, third_res, prints, old, new)
    residual, owner_new = lax.optimization_barrier((residual, owner_new))
    traces_new = owner_new.reshape(time_count * frames, owned).T
    return residual.transpose(0, 2, 1), traces_new


def solution(mesh):
    return jax.shard_map(
        body,
        mesh=mesh,
        in_specs=(
            P("tile", None, "tm"),
            P("tile", None, None, None, None),
            P("tile", None),
            P(),
            P(None, "tile", None),
            P(),
            P(("tile", "tm"), None),
            P(),
        ),
        out_specs=(P("tile", None, "tm"), P(("tile", "tm"), None)),
        check_vma=False,
    )
```
